32 devices in a mesh: parts: 1, axial: 8 (over y, x, core), radial: 4 (over z).
Axes of the slice: x: 2, y: 2, z: 4, core: 2. Of those that a mesh axis runs over, the one named last changes fastest.
Arguments:
- inputs: bfloat16 [64, 64, 8192], P(None, 'radial', ('parts', 'axial')), may hold values from -6 to 6
- saved_pre: bfloat16 [64, 64, 8192], P(None, 'radial', ('parts', 'axial')), may hold values from -6 to 6
- cotangent: bfloat16 [64, 64, 8192], P(None, 'radial', ('parts', 'axial')), may hold values from -24 to 24
- pointwise_weight: bfloat16 [64, 64], replicated, may hold values from -0.75 to 0.75
- spectral_weight: bfloat16 [32, 256, 64, 128], P('radial', 'axial'), may hold values from -3 to 3
Outputs:
- input_grad: bfloat16 [64, 64, 8192], P(None, 'radial', ('parts', 'axial'))
- spectral_grad: float32 [32, 256, 64, 128], P('radial', ('parts', 'axial'))
- weight_grad: float32 [64, 64], P('parts')
The draws below stay inside these ranges and needn't reach their ends.
All inputs are finite; a program needn't handle non-finite values.
Results may differ from the reference program's by a relative error of at most 0.0053.
Values may be sent and summed in bfloat16 or wider, within the bound.
No kernel may reach another device: no remote copies, remote signals or barrier semaphores. Data moves between devices by JAX's collectives and lax.ppermute only.
A program may use at most 128 MiB of HBM per device.

```python
import math
import jax
import jax.numpy as jnp
from jax import lax

C = 64
KA = 256
KR = 32
AX_DEV = 1024
RADIAL = 64
AXIAL = 8192
N_AXIAL = 8


def draw_cotangent(key, part):
    axial_ramp = 1.0 + 2.0 * jnp.arange(AXIAL, dtype=jnp.float32) / max(AXIAL - 1, 1)
    radial_ramp = 1.0 + jnp.arange(RADIAL, dtype=jnp.float32) / max(RADIAL - 1, 1)
    envelope = radial_ramp[None, :, None] * axial_ramp[None, None, :]
    base = jnp.clip(jax.random.normal(key, (C, RADIAL, AXIAL), jnp.float32), -4.0, 4.0)
    return (base * envelope).astype(jnp.bfloat16)


def steps_of(own_key, shape, pieces, least, high):
    factor_of, own = 1.0, jax.random.fold_in(own_key, 6)
    for axis_at, parts in pieces:
        draws = jnp.exp(jax.random.uniform(jax.random.fold_in(own, axis_at), (parts,), jnp.float32, least / len(pieces), high / len(pieces)))
        factor_of = factor_of * jnp.repeat(draws, shape[axis_at] // parts).reshape([-1 if axis == axis_at else 1 for axis in range(len(shape))])
    return factor_of


def centred(rng, shape, scale, bound, cuts=(), kind=jnp.bfloat16):
    array = scale * jax.random.normal(rng, shape, jnp.float32)
    if cuts:
        array = array * steps_of(rng, shape, cuts, -0.22, 0.18)
    return jnp.clip(array, -bound, bound).astype(kind)


def setup_inputs(seed: int = 0, part: int = 0) -> dict:
    splits = jax.random.split(jax.random.key(seed), 6)
    part_keys = jax.random.split(jax.random.fold_in(splits[5], part), 6)
    inputs = centred(part_keys[0], (C, RADIAL, AXIAL), 1.0, 6.0, ((1, 4), (2, 8)))
    saved_pre = centred(part_keys[1], (C, RADIAL, AXIAL), 1.0, 6.0, ((1, 4), (2, 8)))
    cotangent = draw_cotangent(jax.random.fold_in(jax.random.fold_in(splits[5], part), 71), part)
    pointwise_weight = centred(splits[3], (C, C), C ** -0.5, 0.75)
    spectral_weight = centred(splits[4], (KR, KA, C, 2 * C), 0.5, 3.0, ((0, 4), (1, 8)))
    return {"inputs": inputs, "saved_pre": saved_pre, "cotangent": cotangent, "pointwise_weight": pointwise_weight, "spectral_weight": spectral_weight}


def axial_table(first, count, modes, total):
    points = first + jnp.arange(count, dtype=jnp.int32)
    orders = jnp.arange(modes, dtype=jnp.int32)
    phase = (points[:, None] * orders[None, :] % total).astype(jnp.float32) * (2.0 * math.pi / total)
    return jnp.stack([jnp.cos(phase), -jnp.sin(phase)], axis=2).reshape(count, 2 * modes).astype(jnp.bfloat16)

def radial_table(first, count, rows_first, rows_count, kept, total):
    orders = first + jnp.arange(count, dtype=jnp.int32)
    freqs = orders + jnp.where(orders >= kept // 2, total - kept, 0).astype(jnp.int32)
    rows = rows_first + jnp.arange(rows_count, dtype=jnp.int32)
    phase = (freqs[:, None] * rows[None, :] % total).astype(jnp.float32) * (2.0 * math.pi / total)
    return (jnp.cos(phase), jnp.sin(phase))

def gelu_slope(pre):
    value = pre.astype(jnp.float32)
    return 0.5 * (1.0 + jax.scipy.special.erf(value / math.sqrt(2.0))) + value * jnp.exp(-0.5 * value * value) / math.sqrt(2.0 * math.pi)

def spectrum(field):

    def step_fn(total, block):
        start = (block * AX_DEV).astype(jnp.int32)
        segment = lax.dynamic_slice_in_dim(field, start, AX_DEV, 2).astype(jnp.float32)
        table = axial_table(start, AX_DEV, KA, AXIAL).astype(jnp.float32)
        part = jnp.einsum('cra,aj->jcr', segment, table, precision=lax.Precision.HIGHEST)
        return (total + part, None)
    start_sum = jnp.zeros((2 * KA, C, RADIAL), jnp.float32)
    total, unused = lax.scan(step_fn, start_sum, jnp.arange(N_AXIAL, dtype=jnp.int32))
    return total

def to_modes(axial_part, cos_r, sin_r):
    split = axial_part.reshape(KA, 2, C, RADIAL)
    real_in = split[:, 0]
    imag_in = split[:, 1]
    high = lax.Precision.HIGHEST
    real_out = jnp.einsum('qr,kcr->qkc', cos_r, real_in, precision=high) + jnp.einsum('qr,kcr->qkc', sin_r, imag_in, precision=high)
    imag_out = jnp.einsum('qr,kcr->qkc', cos_r, imag_in, precision=high) - jnp.einsum('qr,kcr->qkc', sin_r, real_in, precision=high)
    return (real_out, imag_out)

def reference(inputs, saved_pre, cotangent, pointwise_weight, spectral_weight):
    high = lax.Precision.HIGHEST
    grad_pre = (cotangent.astype(jnp.float32) * gelu_slope(saved_pre)).astype(jnp.bfloat16)
    cos_r, sin_r = radial_table(0, KR, 0, RADIAL, KR, RADIAL)
    x_real, x_imag = to_modes(spectrum(inputs), cos_r, sin_r)
    g_real, g_imag = to_modes(spectrum(grad_pre), cos_r, sin_r)
    orders = jnp.arange(KA, dtype=jnp.int32)
    scales = jnp.where(orders == 0, 1.0, 2.0).astype(jnp.float32) / (RADIAL * AXIAL)
    dy_real = g_real * scales[None, :, None]
    dy_imag = g_imag * scales[None, :, None]
    grad_real = x_real[..., :, None] * dy_real[..., None, :] + x_imag[..., :, None] * dy_imag[..., None, :]
    grad_imag = x_real[..., :, None] * dy_imag[..., None, :] - x_imag[..., :, None] * dy_real[..., None, :]
    spectral_grad = jnp.concatenate([grad_real, grad_imag], axis=3)
    w_real = spectral_weight[..., :C].astype(jnp.float32)
    w_imag = spectral_weight[..., C:].astype(jnp.float32)
    dx_real = jnp.einsum('qkio,qko->qki', w_real, dy_real, precision=high) + jnp.einsum('qkio,qko->qki', w_imag, dy_imag, precision=high)
    dx_imag = jnp.einsum('qkio,qko->qki', w_real, dy_imag, precision=high) - jnp.einsum('qkio,qko->qki', w_imag, dy_real, precision=high)
    back_real = jnp.einsum('qr,qkc->kcr', cos_r, dx_real, precision=high) - jnp.einsum('qr,qkc->kcr', sin_r, dx_imag, precision=high)
    back_imag = jnp.einsum('qr,qkc->kcr', sin_r, dx_real, precision=high) + jnp.einsum('qr,qkc->kcr', cos_r, dx_imag, precision=high)
    back = jnp.stack([back_real, back_imag], axis=1).astype(jnp.bfloat16).reshape(2 * KA, C, RADIAL)
    table = axial_table(0, AXIAL, KA, AXIAL).astype(jnp.float32)
    spectral_part = jnp.einsum('jcr,aj->cra', back.astype(jnp.float32), table, precision=high)
    flat_grad = grad_pre.astype(jnp.float32).reshape(C, RADIAL * AXIAL)
    flat_in = inputs.astype(jnp.float32).reshape(C, RADIAL * AXIAL)
    point_part = jnp.dot(pointwise_weight.astype(jnp.float32), flat_grad, precision=high)
    input_grad = (point_part + spectral_part.reshape(C, RADIAL * AXIAL)).astype(jnp.bfloat16).reshape(C, RADIAL, AXIAL)
    weight_grad = jnp.dot(flat_in, flat_grad.T, precision=high) / math.sqrt(RADIAL * AXIAL)
    return (input_grad, spectral_grad, weight_grad)
```

```python
import functools
import math

import jax
import jax.numpy as jnp
import ml_dtypes
import numpy as np
from jax import lax
from jax.experimental import pallas as pl
from jax.experimental.pallas import tpu as pltpu
from jax.sharding import PartitionSpec as P

KA = 256
KR = 32
F32 = jnp.float32
BF16 = jnp.bfloat16
ANYSPACE = pl.ANY


def dot(a, b, dims=((1,), (0,))):
    return lax.dot_general(a, b, (dims, ((), ())), preferred_element_type=F32)


def tree_sum(values):
    while len(values) > 1:
        values = [values[i] + values[i + 1] for i in range(0, len(values), 2)]
    return values[0]


def split(value):
    high = value.astype(BF16)
    return high, (value - high.astype(F32)).astype(BF16)


class Sizes:
    def __init__(self, channels, rows, cols, n_axial, n_radial):
        self.c, self.r, self.a = channels, rows, cols
        self.n_axial, self.n_radial = n_axial, n_radial
        self.chips = n_axial // 2
        self.own = KA // n_axial
        self.j = 2 * self.own
        self.cr = channels * rows
        self.qo = KR // n_radial
        self.cg = 128 // self.qo
        self.ng = channels // self.cg
        self.kb = self.cg * rows
        self.half = KR * self.cg
        self.lanes = self.qo * channels
        self.blk = 256
        self.nblk = self.cr // self.blk
        self.axial_total = cols * n_axial
        self.radial_total = rows * n_radial
        self.ride_a = 16
        self.ride_b = channels * 128 // self.lanes


def axial_base(z):
    k = np.arange(KA, dtype=np.int64)
    a = np.arange(z.a, dtype=np.int64)
    m = (k[:, None] * a[None, :]) % z.axial_total
    phase = m * (2.0 * np.pi / z.axial_total)
    return np.cos(phase).astype(np.float32), np.sin(phase).astype(np.float32)


def axial_shift(z):
    k = np.arange(KA, dtype=np.int64)
    b = np.arange(z.n_axial, dtype=np.int64)
    m = (b[:, None] * k[None, :]) % z.n_axial
    phase = m * (2.0 * np.pi / z.n_axial)
    out = np.zeros((z.n_axial, KA, 128), np.float32)
    out[:, :, 0] = np.cos(phase)
    out[:, :, 1] = np.sin(phase)
    return out


def radial_freqs(z):
    q = np.arange(KR, dtype=np.int64)
    return q + np.where(q >= KR // 2, z.radial_total - KR, 0)


def radial_base(z):
    g = radial_freqs(z)
    r = np.arange(z.r, dtype=np.int64)
    m = (g[:, None] * r[None, :]) % z.radial_total
    phase = m * (2.0 * np.pi / z.radial_total)
    eye = np.eye(z.cg, dtype=np.float64)
    parts = [
        np.einsum("rq,cd->crqd", f(phase).T, eye).reshape(z.kb, z.half) for f in (np.cos, np.sin)
    ]
    table = np.concatenate(parts, axis=1).astype(np.float32)
    high = table.astype(ml_dtypes.bfloat16)
    low = (table - high.astype(np.float32)).astype(ml_dtypes.bfloat16)
    return high, low


def radial_shift(z):
    g = radial_freqs(z)
    first = np.arange(z.n_radial, dtype=np.int64) * z.r
    m = (first[:, None] * g[None, :]) % z.radial_total
    phase = m * (2.0 * np.pi / z.radial_total)
    out = np.zeros((z.n_radial, z.n_radial, 8, 128), np.float32)
    for row, f in ((0, np.cos), (1, np.sin)):
        lanes = np.repeat(f(phase), z.cg, axis=1)
        out[:, :, row, :] = lanes.reshape(z.n_radial, z.n_radial, 128)
    return out


def lane_sums():
    out = np.zeros((8, 2, 128, 128), np.float32)
    for kk in range(8):
        for h in range(2):
            out[kk, h, :, h * 64 + kk] = 1.0
    return out.reshape(2048, 128).astype(ml_dtypes.bfloat16)


def gelu_slope(value):
    return 0.5 * (1.0 + lax.erf(value * (1.0 / math.sqrt(2.0)))) + value * jnp.exp(
        -0.5 * value * value
    ) * (1.0 / math.sqrt(2.0 * math.pi))


def split_owners(z, idx, part, keep_ref, send_ref, stage):
    for o in range(z.n_axial):
        stage[o] = part[o * z.j : (o + 1) * z.j, :].astype(BF16)
    chip, core = idx[0] // 2, idx[0] % 2
    for d in range(z.chips):
        keep_ref[d, : z.j, :] = stage[(chip ^ d) * 2 + core]
        send_ref[d, : z.j, :] = stage[(chip ^ d) * 2 + (1 - core)]


def grad_kernel(z, idx, cos_ref, sin_ref, shift_ref, pre_ref, cot_ref, g_ref, t_ref, keep_ref, send_ref, stage):
    @pl.when(pl.program_id(0) == 0)
    def _():
        for o in range(z.n_axial):
            rows = pl.ds(o * z.own, z.own)
            c1, s1 = cos_ref[rows, :], sin_ref[rows, :]
            c2, s2 = shift_ref[0, rows, 0:1], shift_ref[0, rows, 1:2]
            t_ref[o * z.j : o * z.j + z.own, :] = (c1 * c2 - s1 * s2).astype(BF16)
            t_ref[o * z.j + z.own : (o + 1) * z.j, :] = (-(s1 * c2 + c1 * s2)).astype(BF16)

    g = (cot_ref[...].astype(F32) * gelu_slope(pre_ref[...].astype(F32))).astype(BF16)
    g_ref[...] = g
    part = dot(t_ref[...], g, ((1,), (1,)))
    split_owners(z, idx, part, keep_ref, send_ref, stage)


def input_kernel(z, idx, t_ref, x_ref, g_ref, keep_ref, send_ref, stage):
    x = x_ref[...]
    part = dot(t_ref[...], x, ((1,), (1,)))
    split_owners(z, idx, part, keep_ref, send_ref, stage)
    cross = dot(x, g_ref[...], ((1,), (1,)))
    row = lax.broadcasted_iota(jnp.int32, cross.shape, 0)
    col = lax.broadcasted_iota(jnp.int32, cross.shape, 1)
    cross = jnp.where(row % z.r == col % z.r, cross, 0.0)
    nc = z.blk // z.r
    cross = jnp.sum(cross.reshape(nc, z.r, z.cr), axis=1)
    high, low = split(cross)
    col = lax.broadcasted_iota(jnp.int32, (z.cr, 128), 0) // z.r
    lane = lax.broadcasted_iota(jnp.int32, (z.cr, 128), 1) % z.c
    pick = (col == lane).astype(F32).astype(BF16)
    both = dot(high, pick) + dot(low, pick)
    ride = high_low(z, both)
    ride = jnp.concatenate([ride[i * 8 : (i + 1) * 8] for i in range(nc // 8)], axis=1)
    ride = jnp.concatenate([ride, jnp.zeros_like(ride)], axis=0).astype(BF16)
    for d in range(z.chips):
        keep_ref[d, z.j :, :] = ride
        send_ref[d, z.j :, :] = ride


def high_low(z, both):
    lane = lax.broadcasted_iota(jnp.int32, both.shape, 1) % 128
    high = both.astype(BF16).astype(F32)
    return jnp.where(lane < z.c, high, both - high)


def fold(block):
    return block + pltpu.roll(block, 64, 1)


def add_kernel(z, ride, keep_ref, recv_ref, own_ref, *send_refs):
    for d, out in enumerate((own_ref,) + send_refs):
        total = keep_ref[d, : z.j, :].astype(F32) + recv_ref[d, : z.j, :].astype(F32)
        out[: z.j, :] = total.astype(out.dtype)
    if ride:
        total = keep_ref[0, z.j :, :].astype(F32) + recv_ref[0, z.j :, :].astype(F32)
        parts = [
            high_low(z, fold(total[:, i * 128 : (i + 1) * 128])) for i in range(z.cr // 128)
        ]
        total = jnp.concatenate(parts, axis=1).astype(BF16)
        for out in (own_ref,) + send_refs:
            out[z.j :, :] = total.astype(out.dtype)


def radial_kernel(z, ride, idx, high_ref, low_ref, shift_ref, *refs):
    pieces, outs, stage = refs[: z.chips], refs[z.chips : z.chips + z.n_radial], refs[-1]
    me = idx[1]
    value = tree_sum([p[: z.j, :].astype(F32) for p in pieces])
    t_high, t_low = high_ref[...], low_ref[...]
    for g in range(z.ng):
        high, low = split(value[:, g * z.kb : (g + 1) * z.kb])
        both = dot(jnp.concatenate([high, low], axis=0), t_high)
        total = both[: z.j] + both[z.j :] + dot(high, t_low)
        c, s = total[:, : z.half], total[:, z.half :]
        real = c[: z.own] + s[z.own :]
        imag = c[z.own :] - s[: z.own]
        for zz in range(z.n_radial):
            cos, sin = shift_ref[0, zz, 0:1, :], shift_ref[0, zz, 1:2, :]
            lanes = slice(zz * 128, (zz + 1) * 128)
            re, im = real[:, lanes], imag[:, lanes]
            stage[zz, : z.own, g * 128 : (g + 1) * 128] = cos * re + sin * im
            stage[zz, z.own : z.j, g * 128 : (g + 1) * 128] = cos * im - sin * re
    for d, out in enumerate(outs):
        out[: z.j, :] = stage[me ^ d].astype(out.dtype)
    if ride:
        total = tree_sum([p[z.j : z.j + 8, :].astype(F32) for p in pieces])
        parts = [
            high_low(z, fold(total[:, i * 128 : (i + 1) * 128])) for i in range(z.cr // 128)
        ]
        w = jnp.concatenate(parts, axis=0)
        n = z.ride_b
        w = jnp.concatenate([w[i * n : (i + 1) * n] for i in range(z.lanes // 128)], axis=1)
        w = w.astype(BF16)
        for out in outs:
            out[z.j :, :] = w.astype(out.dtype)


def channel_rows(z, value):
    if z.j < 128:
        value = jnp.concatenate([value, jnp.zeros((128 - z.j, z.lanes), F32)], axis=0)
    turned = value.T
    blocks = []
    for q in range(z.qo):
        starts = [(g * z.qo + q) * z.cg for g in range(z.ng)]
        blocks.append(jnp.concatenate([turned[s : s + z.cg] for s in starts], axis=0))
    return blocks


def mode_kernel(z, idx, w_ref, e_ref, *refs):
    pieces = refs[: z.n_radial]
    dx_ref, dy_ref, products, acc = refs[z.n_radial :]
    step = pl.program_id(0)

    @pl.when(step == 0)
    def _():
        value = tree_sum([p[...].astype(F32) for p in pieces])
        k = lax.broadcasted_iota(jnp.int32, value.shape, 0) % z.own + idx[0] * z.own
        scale = 1.0 / (z.radial_total * z.axial_total)
        value = value * jnp.where(k == 0, scale, 2.0 * scale)
        blocks = channel_rows(z, value)
        lane = lax.broadcasted_iota(jnp.int32, (z.own, 128), 1)
        for q in range(0, z.qo, 2):
            pair = jnp.concatenate(blocks[q : q + 2], axis=0).T
            re, im = pair[: z.own], pair[z.own : z.j]
            re2, im2 = pltpu.roll(re, 64, 1), pltpu.roll(im, 64, 1)
            dy_ref[q, 0] = jnp.where(lane < 64, re, im2)
            dy_ref[q, 1] = jnp.where(lane < 64, im, -re2)
            dy_ref[q + 1, 0] = jnp.where(lane < 64, re2, im)
            dy_ref[q + 1, 1] = jnp.where(lane < 64, im2, -re)
        acc[...] = jnp.zeros_like(acc)

    for q in range(z.qo):
        for kk in range(8):
            w = w_ref[q, kk].astype(F32)
            d0 = dy_ref[q, 0, pl.ds(step * 8 + kk, 1), :]
            d1 = dy_ref[q, 1, pl.ds(step * 8 + kk, 1), :]
            rows = slice(q * z.c, (q + 1) * z.c)
            products[rows, kk * 256 : kk * 256 + 128] = (w * d0).astype(BF16)
            products[rows, kk * 256 + 128 : kk * 256 + 256] = (w * d1).astype(BF16)
    sums = dot(products[...], e_ref[...])
    acc[...] += pltpu.roll(sums, step * 8, 1)

    @pl.when(step == pl.num_programs(0) - 1)
    def _():
        rows = []
        for g in range(z.ng):
            for q in range(z.qo):
                start = q * z.c + g * z.cg
                rows.append(acc[start : start + z.cg, :])
        turned = jnp.concatenate(rows, axis=0).T
        dx_ref[: z.own, :] = turned[: z.own].astype(BF16)
        dx_ref[z.own :, :] = turned[64 : 64 + z.own].astype(BF16)


def outer_kernel(z, dy_ref, *refs):
    pieces = refs[: z.n_radial]
    out_ref, wg_ref, x_rows = refs[z.n_radial :]
    step = pl.program_id(0)

    @pl.when(step == 0)
    def _():
        value = tree_sum([p[: z.j, :].astype(F32) for p in pieces])
        for q, block in enumerate(channel_rows(z, value)):
            x_rows[q] = block
        ride = tree_sum([p[z.j :, :].astype(F32) for p in pieces])
        n = z.lanes // 128
        ride = jnp.concatenate([fold(ride[:, i * 128 : (i + 1) * 128]) for i in range(n)], axis=0)
        wg_ref[...] = ride[:, : z.c] * (1.0 / math.sqrt(z.radial_total * z.axial_total))

    x = x_rows[step]
    for k in range(z.own):
        d0 = dy_ref[0, 0, k : k + 1, :]
        d1 = dy_ref[0, 1, k : k + 1, :]
        out_ref[0, k] = x[:, k : k + 1] * d0 + x[:, z.own + k : z.own + k + 1] * d1


def back_kernel(z, idx, high_ref, low_ref, shift_ref, *refs):
    pieces, (out_ref, stage) = refs[: z.n_radial], refs[z.n_radial :]
    me = idx[1]
    for d, piece in enumerate(pieces):
        zz = me ^ d
        cos, sin = shift_ref[0, zz, 0:1, :], shift_ref[0, zz, 1:2, :]
        for g in range(z.ng):
            block = piece[:, g * 128 : (g + 1) * 128].astype(F32)
            re, im = block[: z.own], block[z.own :]
            stage[zz, g, : z.own, :] = (cos * re - sin * im).astype(BF16)
            stage[zz, g, z.own :, :] = (sin * re + cos * im).astype(BF16)
    cos_high, sin_high = high_ref[:, : z.half], high_ref[:, z.half :]
    cos_low, sin_low = low_ref[:, : z.half], low_ref[:, z.half :]
    nt = ((1,), (1,))
    for g in range(z.ng):
        lhs = jnp.concatenate([stage[zz, g] for zz in range(z.n_radial)], axis=1)
        c = dot(lhs, cos_high, nt) + dot(lhs, cos_low, nt)
        s = dot(lhs, sin_high, nt) + dot(lhs, sin_low, nt)
        lanes = slice(g * z.kb, (g + 1) * z.kb)
        out_ref[: z.own, lanes] = (c[: z.own] - s[z.own :]).astype(BF16)
        out_ref[z.own :, lanes] = (s[: z.own] + c[z.own :]).astype(BF16)


def point_kernel(z, w_ref, g_ref, out_ref):
    n = z.blk // z.r
    row = lax.broadcasted_iota(jnp.int32, (z.blk, n), 0) // z.r
    pick = (row == lax.broadcasted_iota(jnp.int32, (z.blk, n), 1)).astype(F32).astype(BF16)
    tall = dot(pick, w_ref[...]).astype(BF16)
    col = lax.broadcasted_iota(jnp.int32, (z.c, z.cr), 1) // z.r
    pick = (col == lax.broadcasted_iota(jnp.int32, (z.c, z.cr), 0)).astype(F32).astype(BF16)
    full = dot(tall, pick)
    row = lax.broadcasted_iota(jnp.int32, full.shape, 0) % z.r
    col = lax.broadcasted_iota(jnp.int32, full.shape, 1) % z.r
    full = jnp.where(row == col, full, 0.0).astype(BF16)
    out_ref[...] = dot(full, g_ref[...])


def final_kernel(z, idx, t_ref, point_ref, *refs):
    pieces, (out_ref, stage) = refs[: z.n_axial], refs[z.n_axial :]

    @pl.when(pl.program_id(0) == 0)
    def _():
        for d, piece in enumerate(pieces):
            rows = pl.ds(pl.multiple_of((idx[0] ^ d) * z.j, z.j), z.j)
            for b in range(z.nblk):
                stage[b, rows, :] = piece[:, b * z.blk : (b + 1) * z.blk]

    lines = stage[pl.program_id(0)]
    out_ref[...] = (dot(lines, t_ref[...], ((0,), (0,))) + point_ref[...]).astype(BF16)


def whole_spec(shape):
    return pl.BlockSpec(shape, lambda *_: (0,) * len(shape))


def call(kernel, idx, grid, in_specs, out_specs, out_shape, scratch, args, flops, name):
    size = sum(math.prod(s.shape) * s.dtype.itemsize for s in jax.tree.leaves(out_shape))
    size += sum(math.prod(a.shape) * a.dtype.itemsize for a in args)
    return pl.pallas_call(
        kernel,
        out_shape=out_shape,
        grid_spec=pltpu.PrefetchScalarGridSpec(
            num_scalar_prefetch=0 if idx is None else 1,
            grid=grid,
            in_specs=in_specs,
            out_specs=out_specs,
            scratch_shapes=scratch,
        ),
        compiler_params=pltpu.CompilerParams(vmem_limit_bytes=48 << 20),
        cost_estimate=pl.CostEstimate(flops=flops, bytes_accessed=size, transcendentals=0),
        name=name,
    )(*(() if idx is None else (idx,)), *args)


def xor_permute(value, axis, size, d):
    return lax.ppermute(value, axis, [(i, i ^ d) for i in range(size)])


def body(inputs, saved_pre, cotangent, pointwise_weight, spectral_weight):
    channels, rows, cols = inputs.shape
    z = Sizes(channels, rows, cols, lax.axis_size("axial"), lax.axis_size("radial"))
    sds = jax.ShapeDtypeStruct
    idx = jnp.stack([lax.axis_index("axial"), lax.axis_index("radial")]).astype(jnp.int32)
    flat = (z.cr, z.a)
    x, pre, cot = (v.reshape(flat) for v in (inputs, saved_pre, cotangent))
    cos_a, sin_a = axial_base(z)
    r_high, r_low = radial_base(z)
    r_shift = radial_shift(z)
    row_block = pl.BlockSpec((z.blk, z.a), lambda i, *_: (i, 0))
    shift_block = pl.BlockSpec((1, z.n_radial, 8, 128), lambda i, idx: (idx[1], 0, 0, 0))

    def part_spec(extra):
        return pl.BlockSpec((z.chips, z.j + extra, z.blk), lambda i, *_: (0, 0, i))

    def part_shape(extra):
        return sds((z.chips, z.j + extra, z.cr), BF16)

    stage = [pltpu.VMEM((z.n_axial, z.j, z.blk), BF16)]
    mm = 2 * KA * z.cr * z.a * 2
    g, table, g_keep, g_send = call(
        functools.partial(grad_kernel, z), idx, (z.nblk,),
        [whole_spec(cos_a.shape), whole_spec(sin_a.shape),
         pl.BlockSpec((1, KA, 128), lambda i, idx: (idx[0], 0, 0)), row_block, row_block],
        [row_block, whole_spec((2 * KA, z.a)), part_spec(0), part_spec(0)],
        [sds(flat, BF16), sds((2 * KA, z.a), BF16), part_shape(0), part_shape(0)],
        stage, (jnp.asarray(cos_a), jnp.asarray(sin_a), jnp.asarray(axial_shift(z)), pre, cot),
        mm * 3, "grad_axial")

    def add(keep, recv, extra, name):
        shape = (z.j + extra, z.cr)
        return call(
            functools.partial(add_kernel, z, extra > 0), None, (1,),
            [whole_spec(keep.shape)] * 2, [whole_spec(shape)] * z.chips,
            [sds(shape, F32)] + [sds(shape, BF16)] * (z.chips - 1), [], (keep, recv), 0, name)

    def axial_exchange(parts):
        return [parts[0]] + [
            xor_permute(parts[d], "axial", z.n_axial, 2 * d) for d in range(1, z.chips)]

    def radial(pieces, extra_in, extra_out, name):
        shape = (z.j + extra_out, z.lanes)
        return call(
            functools.partial(radial_kernel, z, extra_in > 0), idx, (1,),
            [whole_spec(r_high.shape)] * 2 + [shift_block]
            + [whole_spec((z.j + extra_in, z.cr))] * z.chips,
            [whole_spec(shape)] * z.n_radial,
            [sds(shape, F32)] + [sds(shape, BF16)] * (z.n_radial - 1),
            [pltpu.VMEM((z.n_radial, z.j, z.lanes), F32)],
            (jnp.asarray(r_high), jnp.asarray(r_low), jnp.asarray(r_shift), *pieces),
            mm // 2, name)

    def radial_exchange(parts):
        return [parts[0]] + [
            xor_permute(parts[d], "radial", z.n_radial, d) for d in range(1, z.n_radial)]

    g_recv = xor_permute(g_send, "axial", z.n_axial, 1)
    x_keep, x_send = call(
        functools.partial(input_kernel, z), idx, (z.nblk,),
        [whole_spec((2 * KA, z.a)), row_block, whole_spec(flat)],
        [part_spec(z.ride_a)] * 2, [part_shape(z.ride_a)] * 2, stage, (table, x, g),
        mm * 3, "input_axial")
    g_parts = add(g_keep, g_recv, 0, "grad_add")
    g_pieces = axial_exchange(g_parts)
    x_recv = xor_permute(x_send, "axial", z.n_axial, 1)
    point = call(
        functools.partial(point_kernel, z), None, (z.nblk,),
        [pl.BlockSpec((z.blk // z.r, z.c), lambda i: (i, 0)), whole_spec(flat)],
        row_block, sds(flat, F32), [], (pointwise_weight, g), mm * 2, "pointwise")
    x_parts = add(x_keep, x_recv, z.ride_a, "input_add")

    g_modes = radial_exchange(radial(g_pieces, 0, 0, "grad_radial"))
    x_pieces = axial_exchange(x_parts)
    x_own = radial(x_pieces, z.ride_a, z.ride_b, "input_radial")

    piece_shape = (z.j, z.lanes)
    sums = lane_sums()
    d_x, d_y = call(
        functools.partial(mode_kernel, z), idx, (z.own // 8,),
        [pl.BlockSpec((z.qo, 8, z.c, 128), lambda i, *_: (0, i, 0, 0)), whole_spec(sums.shape)]
        + [whole_spec(piece_shape)] * z.n_radial,
        [whole_spec(piece_shape), whole_spec((z.qo, 2, z.own, 128))],
        [sds(piece_shape, BF16), sds((z.qo, 2, z.own, 128), F32)],
        [pltpu.VMEM((z.qo * z.c, 2048), BF16), pltpu.VMEM((z.qo * z.c, 128), F32)],
        (spectral_weight, jnp.asarray(sums), *g_modes), mm * 2, "mode_grad")
    d_pieces = radial_exchange([d_x] * z.n_radial)
    x_modes = radial_exchange(x_own)
    lines = call(
        functools.partial(back_kernel, z), idx, (1,),
        [whole_spec(r_high.shape)] * 2 + [shift_block] + [whole_spec(piece_shape)] * z.n_radial,
        whole_spec((z.j, z.cr)), sds((z.j, z.cr), BF16),
        [pltpu.VMEM((z.n_radial, z.ng, z.j, 128), BF16)],
        (jnp.asarray(r_high), jnp.asarray(r_low), jnp.asarray(r_shift), *d_pieces),
        mm // 2, "back_radial")
    near = [lines] + [xor_permute(lines, "axial", z.n_axial, 2 * d) for d in range(1, z.chips)]
    far = [xor_permute(v, "axial", z.n_axial, 1) for v in near]
    all_lines = [v for pair in zip(near, far) for v in pair]
    ride_shape = (z.j + z.ride_b, z.lanes)
    spectral_grad, weight_grad = call(
        functools.partial(outer_kernel, z), None, (z.qo,),
        [pl.BlockSpec((1, 2, z.own, 128), lambda i: (i, 0, 0, 0))]
        + [whole_spec(ride_shape)] * z.n_radial,
        [pl.BlockSpec((1, z.own, z.c, 128), lambda i: (i, 0, 0, 0)), whole_spec((z.c, z.c))],
        [sds((z.qo, z.own, z.c, 128), F32), sds((z.c, z.c), F32)],
        [pltpu.VMEM((z.qo, z.c, 128), F32)], (d_y, *x_modes), mm, "spectral_outer")
    input_grad = call(
        functools.partial(final_kernel, z), idx, (z.nblk,),
        [whole_spec((2 * KA, z.a)), row_block] + [whole_spec((z.j, z.cr))] * z.n_axial,
        row_block, sds(flat, BF16), [pltpu.VMEM((z.nblk, 2 * KA, z.blk), BF16)],
        (table, point, *all_lines), mm, "final_axial")
    return (input_grad.reshape(inputs.shape), spectral_grad, weight_grad)


def solution(mesh):
    placed = (
        P(None, "radial", ("parts", "axial")),
        P(None, "radial", ("parts", "axial")),
        P(None, "radial", ("parts", "axial")),
        P(),
        P("radial", "axial", None, None),
    )
    return jax.shard_map(
        body,
        mesh=mesh,
        in_specs=placed,
        out_specs=(
            P(None, "radial", ("parts", "axial")),
            P("radial", ("parts", "axial"), None, None),
            P("parts", None),
        ),
        check_vma=False,
    )
```

```python
import functools
import math

import jax
import jax.numpy as jnp
import ml_dtypes
import numpy as np
from jax import lax
from jax.experimental import pallas as pl
from jax.experimental.pallas import tpu as pltpu
from jax.sharding import PartitionSpec as P

KA = 256
KR = 32
F32 = jnp.float32
BF16 = jnp.bfloat16


def dot(a, b, dims=((1,), (0,))):
    return lax.dot_general(a, b, (dims, ((), ())), preferred_element_type=F32)


def tree_sum(values):
    while len(values) > 1:
        values = [values[i] + values[i + 1] for i in range(0, len(values), 2)]
    return values[0]


def split(value):
    high = value.astype(BF16)
    return high, (value - high.astype(F32)).astype(BF16)


class Sizes:
    def __init__(self, channels, rows, cols, n_axial, n_radial):
        self.c, self.r, self.a = channels, rows, cols
        self.n_axial, self.n_radial = n_axial, n_radial
        self.chips = n_axial // 2
        self.own = KA // n_axial
        self.j = 2 * self.own
        self.cr = channels * rows
        self.qo = KR // n_radial
        self.cg = 128 // self.qo
        self.ng = channels // self.cg
        self.kb = self.cg * rows
        self.half = KR * self.cg
        self.lanes = self.qo * channels
        self.blk = 256
        self.nblk = self.cr // self.blk
        self.axial_total = cols * n_axial
        self.radial_total = rows * n_radial
        self.ride = 8
        self.ride_b = channels * 128 // self.lanes


def axial_base(z):
    k = np.arange(KA, dtype=np.int64)
    a = np.arange(128, dtype=np.int64)
    m = (k[:, None] * a[None, :]) % z.axial_total
    phase = m * (2.0 * np.pi / z.axial_total)
    return np.stack([np.cos(phase), np.sin(phase)]).astype(np.float32)


def axial_shift(z):
    k = np.arange(KA, dtype=np.int64)
    n = z.a // 128
    first = np.arange(z.n_axial * n, dtype=np.int64).reshape(z.n_axial, n) * 128
    m = (first[:, :, None] * k) % z.axial_total
    phase = m * (2.0 * np.pi / z.axial_total)
    return np.concatenate([np.cos(phase), np.sin(phase)], axis=1).astype(np.float32)


def radial_freqs(z):
    q = np.arange(KR, dtype=np.int64)
    return q + np.where(q >= KR // 2, z.radial_total - KR, 0)


def radial_base(z):
    g = radial_freqs(z)
    r = np.arange(z.r, dtype=np.int64)
    m = (g[:, None] * r[None, :]) % z.radial_total
    phase = m * (2.0 * np.pi / z.radial_total)
    eye = np.eye(z.cg, dtype=np.float64)
    parts = [
        np.einsum("rq,cd->crqd", f(phase).T, eye).reshape(z.kb, z.half) for f in (np.cos, np.sin)
    ]
    table = np.concatenate(parts, axis=1).astype(np.float32)
    high = table.astype(ml_dtypes.bfloat16)
    low = (table - high.astype(np.float32)).astype(ml_dtypes.bfloat16)
    return high, low


def radial_shift(z):
    g = radial_freqs(z)
    first = np.arange(z.n_radial, dtype=np.int64) * z.r
    m = (first[:, None] * g[None, :]) % z.radial_total
    phase = m * (2.0 * np.pi / z.radial_total)
    out = np.zeros((z.n_radial, z.n_radial, 8, 128), np.float32)
    for row, f in ((0, np.cos), (1, np.sin)):
        lanes = np.repeat(f(phase), z.cg, axis=1)
        out[:, :, row, :] = lanes.reshape(z.n_radial, z.n_radial, 128)
    return out


def lane_sums():
    out = np.zeros((8, 2, 128, 128), np.float32)
    for kk in range(8):
        for h in range(2):
            out[kk, h, :, h * 64 + kk] = 1.0
    return out.reshape(2048, 128).astype(ml_dtypes.bfloat16)


def gelu_slope(value):
    return 0.5 * (1.0 + lax.erf(value * (1.0 / math.sqrt(2.0)))) + value * jnp.exp(
        -0.5 * value * value
    ) * (1.0 / math.sqrt(2.0 * math.pi))


def split_owners(z, idx, part, keep_ref, send_ref, stage):
    for o in range(z.n_axial):
        stage[o] = part[o * z.j : (o + 1) * z.j, :].astype(BF16)
    chip, core = idx[0] // 2, idx[0] % 2
    for d in range(z.chips):
        keep_ref[d] = stage[(chip ^ d) * 2 + core]
        send_ref[d] = stage[(chip ^ d) * 2 + (1 - core)]


def grad_kernel(z, idx, base_ref, shift_ref, pre_ref, cot_ref, g_ref, t_ref, keep_ref, send_ref, stage):
    step = pl.program_id(0)

    @pl.when(step == 0)
    def _():
        n = z.a // 128
        shift = shift_ref[0]
        shift = jnp.concatenate([shift, jnp.zeros((128 - 2 * n, KA), F32)], axis=0).T
        cos1, sin1 = base_ref[0], base_ref[1]
        for i in range(n):
            cos2, sin2 = shift[:, i : i + 1], shift[:, n + i : n + i + 1]
            real = (cos1 * cos2 - sin1 * sin2).astype(BF16)
            imag = (-(sin1 * cos2 + cos1 * sin2)).astype(BF16)
            lanes = slice(i * 128, (i + 1) * 128)
            for o in range(z.n_axial):
                rows = slice(o * z.own, (o + 1) * z.own)
                t_ref[o * z.j : o * z.j + z.own, lanes] = real[rows]
                t_ref[o * z.j + z.own : (o + 1) * z.j, lanes] = imag[rows]

    g = (cot_ref[...].astype(F32) * gelu_slope(pre_ref[...].astype(F32))).astype(BF16)
    rows = pl.ds(pl.multiple_of(step * z.blk, z.blk), z.blk)
    g_ref[rows, :] = g
    part = dot(t_ref[...], g, ((1,), (1,)))
    split_owners(z, idx, part, keep_ref.at[:, :, rows], send_ref.at[:, :, rows], stage)


def input_kernel(z, idx, t_ref, x_ref, keep_ref, send_ref, stage):
    for b in range(z.nblk):
        rows = slice(b * z.blk, (b + 1) * z.blk)
        part = dot(t_ref[...], x_ref[rows, :], ((1,), (1,)))
        split_owners(z, idx, part, keep_ref.at[:, :, rows], send_ref.at[:, :, rows], stage.at[b])


def weight_kernel(z, x_ref, g_ref, *refs):
    out_ref = refs[-1]
    nc = z.blk // z.r
    row = lax.broadcasted_iota(jnp.int32, (z.blk, z.cr), 0)
    col = lax.broadcasted_iota(jnp.int32, (z.blk, z.cr), 1)
    same = ((row ^ col) & (z.r - 1)) == 0
    col = lax.broadcasted_iota(jnp.int32, (z.cr, 128), 0) // z.r
    lane = lax.broadcasted_iota(jnp.int32, (z.cr, 128), 1) & (z.c - 1)
    pick = (col == lane).astype(F32).astype(BF16)
    sums = []
    for b in range(z.nblk):
        cross = dot(x_ref[b * z.blk : (b + 1) * z.blk, :], g_ref[...], ((1,), (1,)))
        cross = jnp.where(same, cross, 0.0)
        sums.append(jnp.sum(cross.reshape(nc, z.r, z.cr), axis=1))
    high, low = split(jnp.concatenate(sums, axis=0))
    w = high_low(z, dot(high, pick) + dot(low, pick))
    w = [w[i * 8 : (i + 1) * 8] for i in range(z.cr // 128)]
    out_ref[...] = jnp.concatenate(w, axis=1).astype(BF16)


def high_low(z, both):
    lane = lax.broadcasted_iota(jnp.int32, both.shape, 1) & 127
    high = both.astype(BF16).astype(F32)
    return jnp.where(lane < z.c, high, both - high)


def fold(block):
    return block + pltpu.roll(block, 64, 1)


def fold_all(z, value):
    n = value.shape[1] // 128
    return [high_low(z, fold(value[:, i * 128 : (i + 1) * 128])) for i in range(n)]


def add_kernel(z, keep_ref, recv_ref, *refs):
    outs = refs[-z.chips :]
    for d, out in enumerate(outs):
        total = keep_ref[d].astype(F32) + recv_ref[d].astype(F32)
        out[: z.j, :] = total.astype(out.dtype)
        if out.shape[0] > z.j:
            out[z.j :, :] = refs[0][...].astype(out.dtype)


def radial_kernel(z, idx, high_ref, low_ref, shift_ref, *refs):
    pieces, outs, stage = refs[: z.chips], refs[-1 - z.n_radial : -1], refs[-1]
    me = idx[1]
    value = tree_sum([p[: z.j, :].astype(F32) for p in pieces])
    for g in range(z.ng):
        high, low = split(value[:, g * z.kb : (g + 1) * z.kb])
        both = dot(jnp.concatenate([high, low], axis=0), high_ref[...])
        total = both[: z.j] + both[z.j :] + dot(high, low_ref[...])
        c, s = total[:, : z.half], total[:, z.half :]
        real = c[: z.own] + s[z.own :]
        imag = c[z.own :] - s[: z.own]
        for zz in range(z.n_radial):
            cos, sin = shift_ref[me, zz, 0:1, :], shift_ref[me, zz, 1:2, :]
            lanes = slice(zz * 128, (zz + 1) * 128)
            re, im = real[:, lanes], imag[:, lanes]
            stage[zz, : z.own, g * 128 : (g + 1) * 128] = cos * re + sin * im
            stage[zz, z.own : z.j, g * 128 : (g + 1) * 128] = cos * im - sin * re
    for d, out in enumerate(outs):
        out[: z.j, :] = stage[me ^ d].astype(out.dtype)
    if outs[0].shape[0] > z.j:
        w, n = tree_sum([p[z.j :, :].astype(F32) for p in pieces]), z.ride_b
        w = jnp.concatenate(fold_all(z, w), axis=0)
        w = jnp.concatenate([w[i * n : (i + 1) * n] for i in range(z.lanes // 128)], axis=1)
        w = w.astype(BF16)
        for out in outs:
            out[z.j :, :] = w.astype(out.dtype)


def channel_rows(z, value):
    if z.j < 128:
        value = jnp.concatenate([value, jnp.zeros((128 - z.j, z.lanes), F32)], axis=0)
    turned = value.T
    blocks = []
    for q in range(z.qo):
        starts = [(g * z.qo + q) * z.cg for g in range(z.ng)]
        blocks.append(jnp.concatenate([turned[s : s + z.cg] for s in starts], axis=0))
    return blocks


def mode_kernel(z, idx, w_ref, e_ref, *refs):
    pieces = refs[: z.n_radial]
    dx_ref, dy_ref, even, odd, acc = refs[-5:]
    value = tree_sum([p[...].astype(F32) for p in pieces])
    k = (lax.broadcasted_iota(jnp.int32, value.shape, 0) & (z.own - 1)) + idx[0] * z.own
    scale = 1.0 / (z.radial_total * z.axial_total)
    value = value * jnp.where(k == 0, scale, 2.0 * scale)
    blocks = channel_rows(z, value)
    lane = lax.broadcasted_iota(jnp.int32, (z.own, 128), 1)
    for q in range(0, z.qo, 2):
        pair = jnp.concatenate(blocks[q : q + 2], axis=0).T
        re, im = pair[: z.own], pair[z.own : z.j]
        re2, im2 = pltpu.roll(re, 64, 1), pltpu.roll(im, 64, 1)
        dy_ref[q, 0] = jnp.where(lane < 64, re, im2)
        dy_ref[q, 1] = jnp.where(lane < 64, im, -re2)
        dy_ref[q + 1, 0] = jnp.where(lane < 64, re2, im)
        dy_ref[q + 1, 1] = jnp.where(lane < 64, im2, -re)
    total = None
    for i in range(z.own // 8):
        products = even if i % 2 == 0 else odd
        for q in range(z.qo):
            rows = slice(q * z.c, (q + 1) * z.c)
            for kk in range(8):
                k = i * 8 + kk
                w = w_ref[q, k].astype(F32)
                d0 = dy_ref[q, 0, k : k + 1, :]
                d1 = dy_ref[q, 1, k : k + 1, :]
                products[rows, kk * 256 : kk * 256 + 128] = (w * d0).astype(BF16)
                products[rows, kk * 256 + 128 : kk * 256 + 256] = (w * d1).astype(BF16)
        sums = dot(products[...], e_ref[...])
        sums = pltpu.roll(sums, i * 8, 1) if i else sums
        total = sums if total is None else total + sums
    acc[...] = total
    rows = []
    for g in range(z.ng):
        for q in range(z.qo):
            start = q * z.c + g * z.cg
            rows.append(acc[start : start + z.cg, :])
    turned = jnp.concatenate(rows, axis=0).T
    dx_ref[: z.own, :] = turned[: z.own].astype(BF16)
    dx_ref[z.own :, :] = turned[64 : 64 + z.own].astype(BF16)


def outer_kernel(z, dy_ref, *refs):
    pieces = refs[: z.n_radial]
    out_ref, w_ref, x_rows = refs[-3:]
    step = pl.program_id(0)

    @pl.when(step == 0)
    def _():
        value = tree_sum([p[: z.j, :].astype(F32) for p in pieces])
        for q, block in enumerate(channel_rows(z, value)):
            high, low = split(block)
            x_rows[q * z.c : (q + 1) * z.c, :128] = high
            x_rows[q * z.c : (q + 1) * z.c, 128:] = low
        w = fold_all(z, tree_sum([p[z.j :, :].astype(F32) for p in pieces]))
        w = jnp.concatenate(w, axis=0)
        w = [w[i * 8 : (i + 1) * 8] for i in range(z.cr // 128)]
        w_ref[...] = jnp.concatenate(w, axis=1)

    row = lax.broadcasted_iota(jnp.int32, (256, 256), 0) & 127
    lane = lax.broadcasted_iota(jnp.int32, (256, 256), 1)
    base = row - jnp.where(lane < 128, 0, z.own)
    for kk in range(8):
        k = step * 8 + kk
        spread = dot(x_rows[...], jnp.where(base == k, 1.0, 0.0).astype(BF16))
        for q in range(z.qo):
            d0 = dy_ref[q, 0, pl.ds(k, 1), :]
            d1 = dy_ref[q, 1, pl.ds(k, 1), :]
            x = spread[q * z.c : (q + 1) * z.c]
            out_ref[q, kk] = x[:, :128] * d0 + x[:, 128:] * d1


def back_kernel(z, idx, high_ref, low_ref, shift_ref, *refs):
    pieces, (out_ref, stage) = refs[: z.n_radial], refs[-2:]
    me = idx[1]
    for d, piece in enumerate(pieces):
        zz = me ^ d
        cos, sin = shift_ref[me, zz, 0:1, :], shift_ref[me, zz, 1:2, :]
        for g in range(z.ng):
            block = piece[:, g * 128 : (g + 1) * 128].astype(F32)
            re, im = block[: z.own], block[z.own :]
            stage[zz, g * z.j : g * z.j + z.own, :] = (cos * re - sin * im).astype(BF16)
            stage[zz, g * z.j + z.own : (g + 1) * z.j, :] = (sin * re + cos * im).astype(BF16)
    nt = ((1,), (1,))
    lhs = jnp.concatenate([stage[zz] for zz in range(z.n_radial)], axis=1)
    c = dot(lhs, high_ref[:, : z.half], nt) + dot(lhs, low_ref[:, : z.half], nt)
    s = dot(lhs, high_ref[:, z.half :], nt) + dot(lhs, low_ref[:, z.half :], nt)
    for g in range(z.ng):
        lanes = slice(g * z.kb, (g + 1) * z.kb)
        re, im = slice(g * z.j, g * z.j + z.own), slice(g * z.j + z.own, (g + 1) * z.j)
        out_ref[: z.own, lanes] = (c[re] - s[im]).astype(BF16)
        out_ref[z.own : z.j, lanes] = (s[re] + c[im]).astype(BF16)


def pack_kernel(z, w_ref, *refs):
    pieces, out_ref = refs[: z.chips], refs[-1]
    for d in range(z.chips):
        out_ref[d * z.j : (d + 1) * z.j, :] = pieces[d][...]
    w = w_ref[...]
    out_ref[KA :, :] = jnp.concatenate([w, jnp.zeros_like(w)], axis=0).astype(BF16)


def pick_table(z, idx, t_ref, stage, far):
    chip, core = idx[0] // 2, idx[0] % 2
    for d in range(z.chips):
        owner = (chip ^ d) * 2 + (1 - core if far else core)
        rows = pl.ds(pl.multiple_of(owner * z.j, z.j), z.j)
        stage[d * z.j : (d + 1) * z.j, :] = t_ref[rows, :]


def near_kernel(z, idx, t_ref, w_ref, g_ref, lines_ref, out_ref, stage):
    pick_table(z, idx, t_ref, stage, False)
    row = lax.broadcasted_iota(jnp.int32, (z.cr, z.c), 0) // z.r
    pick = (row == lax.broadcasted_iota(jnp.int32, (z.cr, z.c), 1)).astype(F32).astype(BF16)
    tall = dot(pick, w_ref[...]).astype(BF16)
    row = lax.broadcasted_iota(jnp.int32, (z.blk, z.cr), 0)
    col = lax.broadcasted_iota(jnp.int32, (z.blk, z.cr), 1)
    same = ((row ^ col) & (z.r - 1)) == 0
    for b in range(z.nblk):
        rows = slice(b * z.blk, (b + 1) * z.blk)
        full = dot(tall[rows], pick, ((1,), (1,)))
        full = jnp.where(same, full, 0.0).astype(BF16)
        near = dot(lines_ref[:KA, rows], stage[...], ((0,), (0,)))
        out_ref[rows, :] = dot(full, g_ref[...]) + near


def final_kernel(z, idx, t_ref, near_ref, pack_ref, lines_ref, out_ref, wg_ref, stage, result, sems):
    pick_table(z, idx, t_ref, stage, True)
    copies = []
    for b in range(z.nblk):
        rows = slice(b * z.blk, (b + 1) * z.blk)
        part = dot(lines_ref[:KA, rows], stage[...], ((0,), (0,)))
        result[b] = (part + near_ref[rows, :]).astype(BF16)
        copies.append(pltpu.make_async_copy(result.at[b], out_ref.at[rows, :], sems.at[b]))
        copies[-1].start()
    w = pack_ref[KA : KA + 8, :].astype(F32) + lines_ref[KA : KA + 8, :].astype(F32)
    w = [fold(w[:, i * 128 : (i + 1) * 128])[:, : z.c] for i in range(z.cr // 128)]
    scale = 1.0 / math.sqrt(z.radial_total * z.axial_total)
    wg_ref[...] = jnp.concatenate(w, axis=0) * scale
    for copy in copies:
        copy.wait()


def whole_spec(shape):
    return pl.BlockSpec(shape, lambda *_: (0,) * len(shape))


VSPEC = pl.BlockSpec(memory_space=pltpu.VMEM)
ASPEC = pl.BlockSpec(memory_space=pl.ANY)


def params(limit):
    return pltpu.CompilerParams(vmem_limit_bytes=limit << 20)


def cost(args, outs, flops):
    size = sum(math.prod(a.shape) * a.dtype.itemsize for a in (*args, *outs))
    return pl.CostEstimate(flops=flops, bytes_accessed=size, transcendentals=0)


def small(kernel, idx, args, outs, scratch, name, flops=0, after=(), out_specs=None, aliases=None):
    head = () if idx is None else (idx,)
    specs = [pl.BlockSpec(memory_space=pltpu.SMEM)] * len(head)
    return pl.pallas_call(
        kernel,
        out_shape=outs,
        in_specs=specs + [VSPEC] * len(args) + [ASPEC] * len(after),
        out_specs=out_specs or [VSPEC] * len(outs),
        scratch_shapes=scratch,
        compiler_params=params(20),
        cost_estimate=cost(args, outs, flops),
        input_output_aliases=aliases or {},
        name=name,
    )(*head, *args, *after)


def xor_permute(value, axis, size, d):
    return lax.ppermute(value, axis, [(i, i ^ d) for i in range(size)])


def body(inputs, saved_pre, cotangent, pointwise_weight, spectral_weight):
    channels, rows, cols = inputs.shape
    z = Sizes(channels, rows, cols, lax.axis_size("axial"), lax.axis_size("radial"))
    sds = jax.ShapeDtypeStruct
    idx = jnp.stack([lax.axis_index("axial"), lax.axis_index("radial")]).astype(jnp.int32)
    flat = (z.cr, z.a)
    x, pre, cot = (v.reshape(flat) for v in (inputs, saved_pre, cotangent))
    base, shift = axial_base(z), axial_shift(z)
    tables = tuple(jnp.asarray(v) for v in (*radial_base(z), radial_shift(z)))
    row_block = pl.BlockSpec((z.blk, z.a), lambda i, *_: (i, 0))
    parts_shape = sds((z.chips, z.j, z.cr), BF16)
    part_spec = pl.BlockSpec((z.chips, z.j, z.blk), lambda i, *_: (0, 0, i))
    mm = 2 * KA * z.cr * z.a * 2
    bind = functools.partial

    grad_out = [sds(flat, BF16), sds((2 * KA, z.a), BF16), parts_shape, parts_shape]
    grad_in = (jnp.asarray(base), jnp.asarray(shift), pre, cot)
    g, table, g_keep, g_send = pl.pallas_call(
        bind(grad_kernel, z),
        out_shape=grad_out,
        grid_spec=pltpu.PrefetchScalarGridSpec(
            num_scalar_prefetch=1,
            grid=(z.nblk,),
            in_specs=[
                whole_spec(base.shape),
                pl.BlockSpec((1,) + shift.shape[1:], lambda i, idx: (idx[0], 0, 0)),
                row_block,
                row_block,
            ],
            out_specs=[VSPEC] * 4,
            scratch_shapes=[pltpu.VMEM((z.n_axial, z.j, z.blk), BF16)],
        ),
        compiler_params=params(48),
        cost_estimate=cost(grad_in, grad_out, mm * 3),
        name="grad_axial",
    )(idx, *grad_in)

    def add(keep, recv, ride, name, after=()):
        shape = (z.j + (z.ride if ride else 0), z.cr)
        outs = [sds(shape, F32)] + [sds(shape, BF16)] * (z.chips - 1)
        return small(bind(add_kernel, z), None, (keep, recv, *ride), outs, [], name, after=after)

    def axial_exchange(parts):
        return [parts[0]] + [
            xor_permute(parts[d], "axial", z.n_axial, 2 * d) for d in range(1, z.chips)]

    def radial(pieces, ride, name, after=()):
        shape = (z.j + ride, z.lanes)
        outs = [sds(shape, F32)] + [sds(shape, BF16)] * (z.n_radial - 1)
        return small(
            bind(radial_kernel, z), idx, (*tables, *pieces), outs,
            [pltpu.VMEM((z.n_radial, z.j, z.lanes), F32)], name, mm // 2, after)

    def radial_exchange(parts):
        return [parts[0]] + [
            xor_permute(parts[d], "radial", z.n_radial, d) for d in range(1, z.n_radial)]

    g_recv = xor_permute(g_send, "axial", z.n_axial, 1)
    x_keep, x_send = small(
        bind(input_kernel, z), idx, (table, x), [parts_shape] * 2,
        [pltpu.VMEM((z.nblk, z.n_axial, z.j, z.blk), BF16)], "input_axial", mm)
    x_recv = xor_permute(x_send, "axial", z.n_axial, 1)
    g_parts = add(g_keep, g_recv, (), "grad_add", (x_keep,))
    g_pieces = axial_exchange(g_parts)
    (weight,) = small(
        bind(weight_kernel, z), None, (x, g), [sds((z.ride, z.cr), BF16)], [], "weight", mm * 2,
        (g_parts[0],))
    g_sends = radial(g_pieces, 0, "grad_radial", (weight,))
    g_modes = radial_exchange(g_sends)
    x_parts = add(x_keep, x_recv, (weight,), "input_add", (g_sends[0],))
    x_pieces = axial_exchange(x_parts)

    piece_shape = (z.j, z.lanes)
    d_x, d_y = small(
        bind(mode_kernel, z), idx, (spectral_weight, jnp.asarray(lane_sums()), *g_modes),
        [sds(piece_shape, BF16), sds((z.qo, 2, z.own, 128), F32)],
        [pltpu.VMEM((z.qo * z.c, 2048), BF16)] * 2 + [pltpu.VMEM((z.qo * z.c, 128), F32)],
        "mode_grad", mm * 2, (x_parts[0],))
    d_pieces = radial_exchange([d_x] * z.n_radial)
    x_sends = radial(x_pieces, z.ride_b, "input_radial", (d_x,))
    x_modes = radial_exchange(x_sends)
    (lines,) = small(
        bind(back_kernel, z), idx, (*tables, *d_pieces), [sds((z.j, z.cr), BF16)],
        [pltpu.VMEM((z.n_radial, z.ng * z.j, 128), BF16)], "back_radial", mm // 2, (x_sends[0],))
    near = [lines] + [xor_permute(lines, "axial", z.n_axial, 2 * d) for d in range(1, z.chips)]
    outer_out = [sds((z.qo, z.own, z.c, 128), F32), sds((z.ride, z.cr), F32)]
    outer_in = (d_y, *x_modes)
    spectral_grad, weight = pl.pallas_call(
        bind(outer_kernel, z),
        out_shape=outer_out,
        grid=(z.own // 8,),
        in_specs=[VSPEC] * len(outer_in) + [ASPEC],
        out_specs=[
            pl.BlockSpec((z.qo, 8, z.c, 128), lambda i: (0, i, 0, 0)),
            VSPEC,
        ],
        scratch_shapes=[pltpu.VMEM((z.qo * z.c, 256), BF16)],
        compiler_params=params(48),
        cost_estimate=cost(outer_in, outer_out, 0),
        name="spectral_outer",
    )(*outer_in, lines)
    half_shape = sds((KA + 16, z.cr), BF16)
    (packed,) = small(bind(pack_kernel, z), None, (weight, *near), [half_shape], [], "pack")
    far = xor_permute(packed, "axial", z.n_axial, 1)
    half_stage = pltpu.VMEM((KA, z.a), BF16)
    (near_sum,) = small(
        bind(near_kernel, z), idx, (table, pointwise_weight, g, packed), [sds(flat, F32)], [half_stage],
        "near_axial", mm // 2)
    input_grad, weight_grad = small(
        bind(final_kernel, z), idx, (table, near_sum, packed, far),
        [sds(flat, BF16), sds((z.c, z.c), F32)],
        [half_stage, pltpu.VMEM((z.nblk, z.blk, z.a), BF16), pltpu.SemaphoreType.DMA((z.nblk,))],
        "final_axial", mm // 2, (), [ASPEC, VSPEC])
    return (input_grad.reshape(inputs.shape), spectral_grad, weight_grad)


def solution(mesh):
    placed = (
        P(None, "radial", ("parts", "axial")),
        P(None, "radial", ("parts", "axial")),
        P(None, "radial", ("parts", "axial")),
        P(),
        P("radial", "axial", None, None),
    )
    return jax.shard_map(
        body,
        mesh=mesh,
        in_specs=placed,
        out_specs=(
            P(None, "radial", ("parts", "axial")),
            P("radial", ("parts", "axial"), None, None),
            P("parts", None),
        ),
        check_vma=False,
    )
```

```python
import functools
import math

import jax
import jax.numpy as jnp
import ml_dtypes
import numpy as np
from jax import lax
from jax.experimental import pallas as pl
from jax.experimental.pallas import tpu as pltpu
from jax.sharding import PartitionSpec as P

KA = 256
KR = 32
F32 = jnp.float32
BF16 = jnp.bfloat16


def dot(a, b, dims=((1,), (0,))):
    return lax.dot_general(a, b, (dims, ((), ())), preferred_element_type=F32)


def tree_sum(values):
    while len(values) > 1:
        values = [values[i] + values[i + 1] for i in range(0, len(values), 2)]
    return values[0]


def split(value):
    high = value.astype(BF16)
    return high, (value - high.astype(F32)).astype(BF16)


class Sizes:
    def __init__(self, channels, rows, cols, n_axial, n_radial):
        self.c, self.r, self.a = channels, rows, cols
        self.n_axial, self.n_radial = n_axial, n_radial
        self.chips = n_axial // 2
        self.own = KA // n_axial
        self.j = 2 * self.own
        self.cr = channels * rows
        self.qo = KR // n_radial
        self.cg = 128 // self.qo
        self.ng = channels // self.cg
        self.kb = self.cg * rows
        self.half = KR * self.cg
        self.lanes = self.qo * channels
        self.blk = 256
        self.nblk = self.cr // self.blk
        self.axial_total = cols * n_axial
        self.radial_total = rows * n_radial
        self.ride = 8
        self.ride_b = channels * channels // self.lanes


def radial_freqs(z):
    q = np.arange(KR, dtype=np.int64)
    return q + np.where(q >= KR // 2, z.radial_total - KR, 0)


def radial_base(z):
    g = radial_freqs(z)
    r = np.arange(z.r, dtype=np.int64)
    m = (g[:, None] * r[None, :]) % z.radial_total
    phase = m * (2.0 * np.pi / z.radial_total)
    eye = np.eye(z.cg, dtype=np.float64)
    parts = [
        np.einsum("rq,cd->crqd", f(phase).T, eye).reshape(z.kb, z.half) for f in (np.cos, np.sin)
    ]
    table = np.concatenate(parts, axis=1).astype(np.float32)
    high = table.astype(ml_dtypes.bfloat16)
    low = (table - high.astype(np.float32)).astype(ml_dtypes.bfloat16)
    return high, low


def radial_shift(z):
    g = radial_freqs(z)
    first = np.arange(z.n_radial, dtype=np.int64) * z.r
    m = (first[:, None] * g[None, :]) % z.radial_total
    phase = m * (2.0 * np.pi / z.radial_total)
    out = np.zeros((z.n_radial, z.n_radial, 8, 128), np.float32)
    for row, f in ((0, np.cos), (1, np.sin)):
        lanes = np.repeat(f(phase), z.cg, axis=1)
        out[:, :, row, :] = lanes.reshape(z.n_radial, z.n_radial, 128)
    return out


def gelu_slope(value):
    return 0.5 * (1.0 + lax.erf(value * (1.0 / math.sqrt(2.0)))) + value * jnp.exp(
        -0.5 * value * value
    ) * (1.0 / math.sqrt(2.0 * math.pi))


def split_owners(z, idx, part, keep_ref, send_ref, stage):
    for o in range(z.n_axial):
        stage[o] = part[o * z.j : (o + 1) * z.j, :].astype(BF16)
    chip, core = idx[0] // 2, idx[0] % 2
    for d in range(z.chips):
        keep_ref[d] = stage[(chip ^ d) * 2 + core]
        send_ref[d] = stage[(chip ^ d) * 2 + (1 - core)]


def turn(m, total):
    u = m.astype(F32) * (math.pi / total)
    v = u * u
    s = jnp.full_like(v, 1.0 / math.factorial(13))
    c = jnp.full_like(v, 1.0 / math.factorial(12))
    for n in range(5, -1, -1):
        s = s * v + (-1) ** n / math.factorial(2 * n + 1)
        c = c * v + (-1) ** n / math.factorial(2 * n)
    s = s * u
    return 1.0 - 2.0 * s * s, 2.0 * s * c


def make_table(z, idx, t_ref):
    k = lax.broadcasted_iota(jnp.int32, (KA, 128), 0)
    lane = lax.broadcasted_iota(jnp.int32, (KA, 128), 1)
    half, mask = z.axial_total // 2, z.axial_total - 1
    cos1, sin1 = turn(((k * lane + half) & mask) - half, z.axial_total)
    shift = k * ((idx[0] * (z.a // 128) + lane) * 128)
    cos2, sin2 = turn(((shift + half) & mask) - half, z.axial_total)
    for i in range(z.a // 128):
        c, s = cos2[:, i : i + 1], sin2[:, i : i + 1]
        real = (cos1 * c - sin1 * s).astype(BF16)
        imag = (-(sin1 * c + cos1 * s)).astype(BF16)
        lanes = slice(i * 128, (i + 1) * 128)
        for o in range(z.n_axial):
            rows = slice(o * z.own, (o + 1) * z.own)
            t_ref[o * z.j : o * z.j + z.own, lanes] = real[rows]
            t_ref[o * z.j + z.own : (o + 1) * z.j, lanes] = imag[rows]


def grad_kernel(z, idx, pre_hbm, cot_hbm, g_ref, t_ref, keep_ref, send_ref, pre_ref, cot_ref, stage, sems):
    copies = []
    for b in range(z.nblk):
        rows = slice(b * z.blk, (b + 1) * z.blk)
        pair = []
        for i, (source, target) in enumerate(((pre_hbm, pre_ref), (cot_hbm, cot_ref))):
            pair.append(pltpu.make_async_copy(source.at[rows, :], target.at[rows, :], sems.at[i, b]))
            pair[-1].start()
        copies.append(pair)
    make_table(z, idx, t_ref)
    for b in range(z.nblk):
        rows = slice(b * z.blk, (b + 1) * z.blk)
        for copy in copies[b]:
            copy.wait()
        slope = gelu_slope(pre_ref[rows, :].astype(F32))
        g = (cot_ref[rows, :].astype(F32) * slope).astype(BF16)
        g_ref[rows, :] = g
        part = dot(t_ref[...], g, ((1,), (1,)))
        split_owners(z, idx, part, keep_ref.at[:, :, rows], send_ref.at[:, :, rows], stage.at[b])


def input_kernel(z, idx, t_ref, x_ref, keep_ref, send_ref, stage):
    for b in range(z.nblk):
        rows = slice(b * z.blk, (b + 1) * z.blk)
        part = dot(t_ref[...], x_ref[rows, :], ((1,), (1,)))
        split_owners(z, idx, part, keep_ref.at[:, :, rows], send_ref.at[:, :, rows], stage.at[b])


def weight_kernel(z, x_ref, g_ref, *refs):
    out_ref = refs[-1]
    nc = z.blk // z.r
    row = lax.broadcasted_iota(jnp.int32, (z.blk, z.cr), 0)
    col = lax.broadcasted_iota(jnp.int32, (z.blk, z.cr), 1)
    same = ((row ^ col) & (z.r - 1)) == 0
    col = lax.broadcasted_iota(jnp.int32, (z.cr, 128), 0) // z.r
    lane = lax.broadcasted_iota(jnp.int32, (z.cr, 128), 1) & (z.c - 1)
    pick = (col == lane).astype(F32).astype(BF16)
    sums = []
    for b in range(z.nblk):
        cross = dot(x_ref[b * z.blk : (b + 1) * z.blk, :], g_ref[...], ((1,), (1,)))
        cross = jnp.where(same, cross, 0.0)
        sums.append(jnp.sum(cross.reshape(nc, z.r, z.cr), axis=1))
    high, low = split(jnp.concatenate(sums, axis=0))
    w = high_low(z, dot(high, pick) + dot(low, pick))
    w = [w[i * 8 : (i + 1) * 8] for i in range(z.cr // 128)]
    out_ref[...] = jnp.concatenate(w, axis=1).astype(BF16)


def high_low(z, both):
    lane = lax.broadcasted_iota(jnp.int32, both.shape, 1) & 127
    high = both.astype(BF16).astype(F32)
    return jnp.where(lane < z.c, high, both - high)


def fold(block):
    return block + pltpu.roll(block, 64, 1)


def fold_all(z, value):
    n = value.shape[1] // 128
    return [high_low(z, fold(value[:, i * 128 : (i + 1) * 128])) for i in range(n)]


def add_kernel(z, keep_ref, recv_ref, *refs):
    outs = refs[-z.chips :]
    for d, out in enumerate(outs):
        total = keep_ref[d].astype(F32) + recv_ref[d].astype(F32)
        out[: z.j, :] = total.astype(out.dtype)
        if out.shape[0] > z.j:
            out[z.j :, :] = refs[0][...].astype(out.dtype)


def radial_kernel(z, idx, high_ref, low_ref, shift_ref, *refs):
    pieces, outs, stage = refs[: z.chips], refs[-1 - z.n_radial : -1], refs[-1]
    me = idx[1]
    value = tree_sum([p[: z.j, :].astype(F32) for p in pieces])
    value = jnp.concatenate([value[:, g * z.kb : (g + 1) * z.kb] for g in range(z.ng)], axis=0)
    high, low = split(value)
    rows = z.ng * z.j
    both = dot(jnp.concatenate([high, low], axis=0), high_ref[...])
    both = both[:rows] + both[rows:] + dot(high, low_ref[...])
    for g in range(z.ng):
        total = both[g * z.j : (g + 1) * z.j]
        c, s = total[:, : z.half], total[:, z.half :]
        real = c[: z.own] + s[z.own :]
        imag = c[z.own :] - s[: z.own]
        for zz in range(z.n_radial):
            cos, sin = shift_ref[me, zz, 0:1, :], shift_ref[me, zz, 1:2, :]
            lanes = slice(zz * 128, (zz + 1) * 128)
            re, im = real[:, lanes], imag[:, lanes]
            stage[zz, : z.own, g * 128 : (g + 1) * 128] = cos * re + sin * im
            stage[zz, z.own : z.j, g * 128 : (g + 1) * 128] = cos * im - sin * re
    for d, out in enumerate(outs):
        out[: z.j, :] = stage[me ^ d].astype(out.dtype)
    if outs[0].shape[0] > z.j:
        w = tree_sum([p[z.j :, :].astype(F32) for p in pieces])
        w = [fold(w[:, i * 128 : (i + 1) * 128]) for i in range(z.cr // 128)]
        w = pair_rows(z, jnp.concatenate(w, axis=0))
        n = w.shape[0] // (z.lanes // 128)
        w = jnp.concatenate([w[i * n : (i + 1) * n] for i in range(z.lanes // 128)], axis=1)
        w = w.astype(BF16)
        for out in outs:
            out[z.j :, :] = w.astype(out.dtype)


def pair_rows(z, w):
    lane = lax.broadcasted_iota(jnp.int32, (z.c // 2, 128), 1)
    return jnp.where(lane < z.c, w[: z.c // 2], w[z.c // 2 :])


def channel_rows(z, value):
    if z.j < 128:
        value = jnp.concatenate([value, jnp.zeros((128 - z.j, z.lanes), F32)], axis=0)
    turned = value.T
    blocks = []
    for q in range(z.qo):
        starts = [(g * z.qo + q) * z.cg for g in range(z.ng)]
        blocks.append(jnp.concatenate([turned[s : s + z.cg] for s in starts], axis=0))
    return blocks


def mode_kernel(z, idx, w_ref, *refs):
    pieces = refs[: z.n_radial]
    dx_ref, dy_ref, acc = refs[-3:]
    value = tree_sum([p[...].astype(F32) for p in pieces])
    k = (lax.broadcasted_iota(jnp.int32, value.shape, 0) & (z.own - 1)) + idx[0] * z.own
    scale = 1.0 / (z.radial_total * z.axial_total)
    value = value * jnp.where(k == 0, scale, 2.0 * scale)
    blocks = channel_rows(z, value)
    lane = lax.broadcasted_iota(jnp.int32, (z.own, 128), 1)
    for q in range(0, z.qo, 2):
        pair = jnp.concatenate(blocks[q : q + 2], axis=0).T
        re, im = pair[: z.own], pair[z.own : z.j]
        re2, im2 = pltpu.roll(re, 64, 1), pltpu.roll(im, 64, 1)
        dy_ref[q, 0] = jnp.where(lane < 64, re, im2)
        dy_ref[q, 1] = jnp.where(lane < 64, im, -re2)
        dy_ref[q + 1, 0] = jnp.where(lane < 64, re2, im)
        dy_ref[q + 1, 1] = jnp.where(lane < 64, im2, -re)
    mode = lax.broadcasted_iota(jnp.int32, (128, 128), 1) & (z.own - 1)
    for q in range(z.qo):
        d = [dy_ref[q, 0], dy_ref[q, 1], jnp.zeros((128 - z.j, 128), F32)]
        d = jnp.concatenate(d, axis=0).T
        right = [jnp.where(mode == k, d, 0.0).astype(BF16) for k in range(z.own)]
        left = jnp.concatenate([w_ref[q, k] for k in range(z.own)], axis=1)
        acc[q * z.c : (q + 1) * z.c, :] = dot(left, jnp.concatenate(right, axis=0))
    rows = []
    for g in range(z.ng):
        for q in range(z.qo):
            start = q * z.c + g * z.cg
            rows.append(acc[start : start + z.cg, :])
    dx_ref[...] = jnp.concatenate(rows, axis=0).T[: z.j].astype(BF16)


def gather_kernel(z, *refs):
    pieces = [refs[0]] + list(refs[1 : z.n_radial])[::-1]
    x_ref, w_ref = refs[-2:]
    value = tree_sum([p[: z.j, :].astype(F32) for p in pieces])
    for q, block in enumerate(channel_rows(z, value)):
        high, low = split(block)
        x_ref[q * z.c : (q + 1) * z.c, :128] = high
        x_ref[q * z.c : (q + 1) * z.c, 128:] = low
    w = tree_sum([p[z.j :, :].astype(F32) for p in pieces])
    w = [w[:, i * 128 : (i + 1) * 128] for i in range(z.lanes // 128)]
    w = jnp.concatenate(split(jnp.concatenate(w, axis=0)), axis=0)
    w_ref[...] = jnp.concatenate([w[i * 8 : (i + 1) * 8] for i in range(z.c // 8)], axis=1)


def outer_kernel(z, idx, dy_ref, x_rows, t_ref, point_ref, lines_ref, grad_ref, near_ref, result, stage, sems):
    row = lax.broadcasted_iota(jnp.int32, (256, 256), 0) & 127
    lane = lax.broadcasted_iota(jnp.int32, (256, 256), 1)
    base = row - jnp.where(lane < 128, 0, z.own)
    copies = []
    for k in range(z.own):
        spread = dot(x_rows[...], jnp.where(base == k, 1.0, 0.0).astype(BF16))
        for q in range(z.qo):
            d0, d1 = dy_ref[q, 0, k : k + 1, :], dy_ref[q, 1, k : k + 1, :]
            x = spread[q * z.c : (q + 1) * z.c]
            result[q, k] = x[:, :128] * d0 + x[:, 128:] * d1
        if k % 4 == 3:
            part = slice(k - 3, k + 1)
            copies.append(
                pltpu.make_async_copy(result.at[:, part], grad_ref.at[:, part], sems.at[k // 4])
            )
            copies[-1].start()
    pick_table(z, idx, t_ref, stage, False)
    for b in range(z.nblk):
        rows = slice(b * z.blk, (b + 1) * z.blk)
        near_ref[rows, :] = dot(lines_ref[:KA, rows], stage[...], ((0,), (0,))) + point_ref[rows, :]
    for copy in copies:
        copy.wait()


def back_kernel(z, idx, high_ref, low_ref, shift_ref, *refs):
    pieces, (out_ref, stage) = refs[: z.n_radial], refs[-2:]
    me = idx[1]
    for d, piece in enumerate(pieces):
        zz = me ^ d
        cos, sin = shift_ref[me, zz, 0:1, :], shift_ref[me, zz, 1:2, :]
        for g in range(z.ng):
            block = piece[:, g * 128 : (g + 1) * 128].astype(F32)
            re, im = block[: z.own], block[z.own :]
            stage[zz, g * z.j : g * z.j + z.own, :] = (cos * re - sin * im).astype(BF16)
            stage[zz, g * z.j + z.own : (g + 1) * z.j, :] = (sin * re + cos * im).astype(BF16)
    nt = ((1,), (1,))
    lhs = jnp.concatenate([stage[zz] for zz in range(z.n_radial)], axis=1)
    c = dot(lhs, high_ref[:, : z.half], nt) + dot(lhs, low_ref[:, : z.half], nt)
    s = dot(lhs, high_ref[:, z.half :], nt) + dot(lhs, low_ref[:, z.half :], nt)
    for g in range(z.ng):
        lanes = slice(g * z.kb, (g + 1) * z.kb)
        re, im = slice(g * z.j, g * z.j + z.own), slice(g * z.j + z.own, (g + 1) * z.j)
        out_ref[: z.own, lanes] = (c[re] - s[im]).astype(BF16)
        out_ref[z.own : z.j, lanes] = (s[re] + c[im]).astype(BF16)


def point_kernel(z, w_ref, g_ref, *refs):
    out_ref = refs[-1]
    row = lax.broadcasted_iota(jnp.int32, (z.cr, z.c), 0) // z.r
    pick = (row == lax.broadcasted_iota(jnp.int32, (z.cr, z.c), 1)).astype(F32).astype(BF16)
    tall = dot(pick, w_ref[...]).astype(BF16)
    row = lax.broadcasted_iota(jnp.int32, (z.blk, z.cr), 0)
    col = lax.broadcasted_iota(jnp.int32, (z.blk, z.cr), 1)
    same = ((row ^ col) & (z.r - 1)) == 0
    for b in range(z.nblk):
        rows = slice(b * z.blk, (b + 1) * z.blk)
        full = dot(tall[rows], pick, ((1,), (1,)))
        full = jnp.where(same, full, 0.0).astype(BF16)
        out_ref[rows, :] = dot(full, g_ref[...])


def pack_kernel(z, w_ref, *refs):
    for d in range(z.chips):
        refs[-1][d * z.j : (d + 1) * z.j, :] = refs[d][...]
    w = w_ref[...]
    refs[-1][KA :, :] = jnp.concatenate([w, jnp.zeros_like(w)], axis=0)


def pick_table(z, idx, t_ref, stage, far):
    chip, core = idx[0] // 2, idx[0] % 2
    for d in range(z.chips):
        owner = (chip ^ d) * 2 + (1 - core if far else core)
        rows = pl.ds(pl.multiple_of(owner * z.j, z.j), z.j)
        stage[d * z.j : (d + 1) * z.j, :] = t_ref[rows, :]


def final_kernel(z, idx, t_ref, near_ref, pack_ref, lines_ref, out_ref, wg_hbm, stage, result, wg_ref, sems):
    w = pack_ref[KA : KA + 8, :].astype(F32) + lines_ref[KA : KA + 8, :].astype(F32)
    w = jnp.concatenate([w[:, i * 128 : (i + 1) * 128] for i in range(z.c // 8)], axis=0)
    w = w[: z.c // 2] + w[z.c // 2 :]
    w = jnp.concatenate([w[:, : z.c], pltpu.roll(w, 64, 1)[:, : z.c]], axis=0)
    wg_ref[...] = w * (1.0 / math.sqrt(z.radial_total * z.axial_total))
    copies = [pltpu.make_async_copy(wg_ref, wg_hbm, sems.at[z.nblk])]
    copies[-1].start()
    pick_table(z, idx, t_ref, stage, True)
    for b in range(z.nblk):
        rows = slice(b * z.blk, (b + 1) * z.blk)
        part = dot(lines_ref[:KA, rows], stage[...], ((0,), (0,)))
        result[b] = (part + near_ref[rows, :]).astype(BF16)
        copies.append(pltpu.make_async_copy(result.at[b], out_ref.at[rows, :], sems.at[b]))
        copies[-1].start()
    for copy in copies:
        copy.wait()


def whole_spec(shape):
    return pl.BlockSpec(shape, lambda *_: (0,) * len(shape))


VSPEC = pl.BlockSpec(memory_space=pltpu.VMEM)
ASPEC = pl.BlockSpec(memory_space=pl.ANY)


def params(limit):
    return pltpu.CompilerParams(vmem_limit_bytes=limit << 20)


def cost(args, outs, flops):
    if flops is None:
        return pl.CostEstimate(flops=0, bytes_accessed=0, transcendentals=0)
    size = sum(math.prod(a.shape) * a.dtype.itemsize for a in (*args, *outs))
    return pl.CostEstimate(flops=flops, bytes_accessed=size, transcendentals=0)


def small(kernel, idx, args, outs, scratch, name, flops=0, after=(), out_specs=None, aliases=None):
    head = () if idx is None else (idx,)
    specs = [pl.BlockSpec(memory_space=pltpu.SMEM)] * len(head)
    return pl.pallas_call(
        kernel,
        out_shape=outs,
        in_specs=specs + [VSPEC] * len(args) + [ASPEC] * len(after),
        out_specs=out_specs or [VSPEC] * len(outs),
        scratch_shapes=scratch,
        compiler_params=params(20),
        cost_estimate=cost(args, outs, flops),
        input_output_aliases=aliases or {},
        name=name,
    )(*head, *args, *after)


def xor_permute(value, axis, size, d):
    return lax.ppermute(value, axis, [(i, i ^ d) for i in range(size)])


def body(inputs, saved_pre, cotangent, pointwise_weight, spectral_weight):
    channels, rows, cols = inputs.shape
    z = Sizes(channels, rows, cols, lax.axis_size("axial"), lax.axis_size("radial"))
    sds = jax.ShapeDtypeStruct
    idx = jnp.stack([lax.axis_index("axial"), lax.axis_index("radial")]).astype(jnp.int32)
    flat = (z.cr, z.a)
    x, pre, cot = (v.reshape(flat) for v in (inputs, saved_pre, cotangent))
    tables = tuple(jnp.asarray(v) for v in (*radial_base(z), radial_shift(z)))
    parts_shape = sds((z.chips, z.j, z.cr), BF16)
    mm = 2 * KA * z.cr * z.a * 2
    bind = functools.partial

    grad_out = [sds(flat, BF16), sds((2 * KA, z.a), BF16), parts_shape, parts_shape]
    g, table, g_keep, g_send = pl.pallas_call(
        bind(grad_kernel, z),
        out_shape=grad_out,
        in_specs=[pl.BlockSpec(memory_space=pltpu.SMEM)] + [ASPEC] * 2,
        out_specs=[VSPEC] * 4,
        scratch_shapes=[
            pltpu.VMEM(flat, BF16),
            pltpu.VMEM(flat, BF16),
            pltpu.VMEM((z.nblk, z.n_axial, z.j, z.blk), BF16),
            pltpu.SemaphoreType.DMA((2, z.nblk)),
        ],
        compiler_params=params(48),
        cost_estimate=cost((pre, cot), grad_out, mm * 3),
        name="grad_axial",
    )(idx, pre, cot)

    def add(keep, recv, ride, name, after=()):
        shape = (z.j + (z.ride if ride else 0), z.cr)
        outs = [sds(shape, F32)] + [sds(shape, BF16)] * (z.chips - 1)
        return small(bind(add_kernel, z), None, (keep, recv, *ride), outs, [], name, after=after)

    def axial_exchange(parts):
        return [parts[0]] + [
            xor_permute(parts[d], "axial", z.n_axial, 2 * d) for d in range(1, z.chips)]

    def radial(pieces, ride, name, after=()):
        shape = (z.j + ride, z.lanes)
        outs = [sds(shape, F32)] + [sds(shape, BF16)] * (z.n_radial - 1)
        return small(
            bind(radial_kernel, z), idx, (*tables, *pieces), outs,
            [pltpu.VMEM((z.n_radial, z.j, z.lanes), F32)], name, mm // 2, after)

    def radial_exchange(parts):
        order = range(z.n_radial - 1, 0, -1)
        moved = {d: xor_permute(parts[d], "radial", z.n_radial, d) for d in order}
        return [parts[0]] + [moved[d] for d in range(1, z.n_radial)]

    g_recv = xor_permute(g_send, "axial", z.n_axial, 1)
    x_keep, x_send = small(
        bind(input_kernel, z), idx, (table, x), [parts_shape] * 2,
        [pltpu.VMEM((z.nblk, z.n_axial, z.j, z.blk), BF16)], "input_axial", mm)
    x_recv = xor_permute(x_send, "axial", z.n_axial, 1)
    g_parts = add(g_keep, g_recv, (), "grad_add", (x_keep,))
    g_pieces = axial_exchange(g_parts)
    (weight,) = small(
        bind(weight_kernel, z), None, (x, g), [sds((z.ride, z.cr), BF16)], [], "weight", mm * 2,
        (g_parts[0],))
    (point,) = small(
        bind(point_kernel, z), None, (pointwise_weight, g), [sds(flat, F32)], [], "pointwise",
        mm * 2, (weight,))
    g_sends = radial(g_pieces, 0, "grad_radial", (point,))
    g_modes = radial_exchange(g_sends)
    x_parts = add(x_keep, x_recv, (weight,), "input_add", (g_sends[0],))
    x_pieces = axial_exchange(x_parts)

    piece_shape = (z.j, z.lanes)
    d_x, d_y = small(
        bind(mode_kernel, z), idx, (spectral_weight, *g_modes),
        [sds(piece_shape, BF16), sds((z.qo, 2, z.own, 128), F32)],
        [pltpu.VMEM((z.qo * z.c, 128), F32)],
        "mode_grad", mm * 2, (x_parts[0],))
    d_pieces = radial_exchange([d_x] * z.n_radial)
    x_sends = radial(x_pieces, z.ride_b, "input_radial", (d_x,))
    x_modes = radial_exchange(x_sends)
    (lines,) = small(
        bind(back_kernel, z), idx, (*tables, *d_pieces), [sds((z.j, z.cr), BF16)],
        [pltpu.VMEM((z.n_radial, z.ng * z.j, 128), BF16)], "back_radial", mm // 2, (x_sends[0],))
    near = [lines] + [xor_permute(lines, "axial", z.n_axial, 2 * d) for d in range(1, z.chips)]
    x_rows, weight = small(
        bind(gather_kernel, z), None, (x_modes[0], *x_modes[:0:-1]),
        [sds((z.qo * z.c, 256), BF16), sds((z.ride, z.c // 8 * 128), BF16)], [], "gather", 0,
        (lines,))
    half_shape = sds((KA + 16, z.cr), BF16)
    (packed,) = small(
        bind(pack_kernel, z), None, (weight, *near), [half_shape], [], "pack", 0, (x_rows,))
    far = xor_permute(packed, "axial", z.n_axial, 1)
    half_stage = pltpu.VMEM((KA, z.a), BF16)
    grad_shape = (z.qo, z.own, z.c, 128)
    spectral_grad, near_sum = small(
        bind(outer_kernel, z), idx, (d_y, x_rows, table, point, packed),
        [sds(grad_shape, F32), sds(flat, F32)],
        [pltpu.VMEM(grad_shape, F32), half_stage, pltpu.SemaphoreType.DMA((z.own // 4,))],
        "spectral_outer", mm, (), [ASPEC, VSPEC])
    input_grad, weight_grad = small(
        bind(final_kernel, z), idx, (table, near_sum, packed, far),
        [sds(flat, BF16), sds((z.c, z.c), F32)],
        [half_stage, pltpu.VMEM((z.nblk, z.blk, z.a), BF16), pltpu.VMEM((z.c, z.c), F32),
         pltpu.SemaphoreType.DMA((z.nblk + 1,))],
        "final_axial", mm // 2, (), [ASPEC, ASPEC])
    return (input_grad.reshape(inputs.shape), spectral_grad, weight_grad)


def solution(mesh):
    placed = (
        P(None, "radial", ("parts", "axial")),
        P(None, "radial", ("parts", "axial")),
        P(None, "radial", ("parts", "axial")),
        P(),
        P("radial", "axial", None, None),
    )
    return jax.shard_map(
        body,
        mesh=mesh,
        in_specs=placed,
        out_specs=(
            P(None, "radial", ("parts", "axial")),
            P("radial", ("parts", "axial"), None, None),
            P("parts", None),
        ),
        check_vma=False,
    )
```
